256 devices in a mesh: group: 16 (over y, x), member: 16 (over z, core).
Axes of the slice: x: 4, y: 4, z: 8, core: 2. Of those that a mesh axis runs over, the one named last changes fastest.
Arguments:
- queries: bfloat16 [65536, 6144], P(('group', 'member')), may hold values from -64 to 64
- keys_values: bfloat16 [512, 128, 2048], P('group', 'member'), may hold values from -8 to 8
- local_lists: int32 [512, 5], P(('group', 'member')), may hold values from -1 to 31, as said below
- remote_lists: int32 [512, 3], P(('group', 'member')), may hold values from -1 to 15, as said below
- send_blocks: int32 [16, 16], P('group'), may hold values from 0 to 31
Outputs:
- attended: bfloat16 [65536, 6144], P(('group', 'member'))
The draws below stay inside these ranges and needn't reach their ends.
Inputs may be any that keep to these rules, and one draw needn't show every extreme that they name: `local_lists`: row i lists distinct blocks of its slab, numbered 0 to 31 within the slab, then -1 in the remaining entries; the first entry is i mod 32, the row's own block. Some row lists 5 blocks. `remote_lists`: row i lists distinct slabs other than its own slab i // 32, then -1 in the remaining entries; a row may list none. Some row lists 3 slabs.
All inputs are finite; a program needn't handle non-finite values.
Results may differ from the reference program's by a relative error of at most 0.0038.
Values may be sent and summed in bfloat16 or wider, within the bound.
A program may use at most 128 MiB of HBM per device.

```python
import jax
import jax.numpy as jnp
from jax import lax

HEADS = 48
KV_HEADS = 8
HEAD_DIM = 128
BLOCK = 128
LOCAL_MOST = 5
REMOTE_MOST = 3
GB = 32
KV_BLOCKS = 512
Q_BLOCKS = 512
TOKENS = 65536
N_GROUP = 16


def draw_base(key):
    base_key = jax.random.fold_in(key, 7)
    shape = (KV_BLOCKS, BLOCK, KV_HEADS * HEAD_DIM)
    keys_part = jax.random.truncated_normal(jax.random.fold_in(base_key, 1), -4.0, 4.0, shape, jnp.float32)
    values_part = 2.0 * jax.random.truncated_normal(jax.random.fold_in(base_key, 2), -4.0, 4.0, shape, jnp.float32)
    return (keys_part, values_part)


def draw_keys_values(key, part):
    keys_part, values_part = draw_base(key)
    return jnp.concatenate([keys_part, values_part], axis=2).astype(jnp.bfloat16)


def draw_queries(key, part):
    total_width = HEADS * HEAD_DIM
    query_key = jax.random.fold_in(key, 3)
    return (1.5 * jax.random.truncated_normal(query_key, -4.0, 4.0, (TOKENS, total_width), jnp.float32)).astype(jnp.bfloat16)


def draw_local_lists(key, part):
    positions = jnp.arange(Q_BLOCKS, dtype=jnp.int32)
    own_block = positions % GB
    row_keys = jax.random.split(jax.random.fold_in(key, 11), Q_BLOCKS)
    picks = jax.vmap(lambda row_key: jax.random.permutation(row_key, GB - 1))(row_keys)[:, :LOCAL_MOST - 1]
    picks = (picks + (picks >= own_block[:, None]).astype(jnp.int32)).astype(jnp.int32)
    entries = jnp.concatenate([own_block[:, None], picks], axis=1)
    first_draw = jax.random.randint(jax.random.fold_in(key, 12), (Q_BLOCKS,), 0, LOCAL_MOST)
    second_draw = jax.random.randint(jax.random.fold_in(key, 13), (Q_BLOCKS,), 0, LOCAL_MOST)
    counts = 1 + first_draw * second_draw // (LOCAL_MOST - 1)
    forced = jax.random.randint(jax.random.fold_in(key, 14), (), 0, Q_BLOCKS)
    counts = jnp.where(positions == forced, LOCAL_MOST, counts)
    slots = jnp.arange(LOCAL_MOST, dtype=jnp.int32)
    return jnp.where(slots[None, :] < counts[:, None], entries, -1).astype(jnp.int32)


def draw_remote_lists(key, part):
    positions = jnp.arange(Q_BLOCKS, dtype=jnp.int32)
    own_group = positions // GB
    row_keys = jax.random.split(jax.random.fold_in(key, 21), Q_BLOCKS)
    picks = jax.vmap(lambda row_key: jax.random.permutation(row_key, N_GROUP - 1))(row_keys)[:, :REMOTE_MOST]
    picks = (picks + (picks >= own_group[:, None]).astype(jnp.int32)).astype(jnp.int32)
    first_draw = jax.random.randint(jax.random.fold_in(key, 22), (Q_BLOCKS,), 0, REMOTE_MOST + 1)
    second_draw = jax.random.randint(jax.random.fold_in(key, 23), (Q_BLOCKS,), 0, REMOTE_MOST + 1)
    counts = first_draw * second_draw // REMOTE_MOST
    forced = jax.random.randint(jax.random.fold_in(key, 24), (), 0, Q_BLOCKS)
    counts = jnp.where(positions == forced, REMOTE_MOST, counts)
    slots = jnp.arange(REMOTE_MOST, dtype=jnp.int32)
    return jnp.where(slots[None, :] < counts[:, None], picks, -1).astype(jnp.int32)


def with_ends(values, stream_key, smallest, top_value):
    longest = values.shape.index(max(values.shape))
    spots = []
    for shift in (0, 1):
        where = [jax.random.randint(jax.random.fold_in(stream_key, axis), (), 0, length) for axis, length in enumerate(values.shape)]
        where[longest] = (where[longest] + shift) % values.shape[longest]
        spots.append(tuple(where))
    return values.at[spots[0]].set(smallest).at[spots[1]].set(top_value)


def setup_inputs(seed: int = 0) -> dict:
    key_of = jax.random.split(jax.random.key(seed), 6)
    queries = draw_queries(jax.random.fold_in(key_of[5], 71), 0)
    keys_values = draw_keys_values(jax.random.fold_in(key_of[5], 71), 0)
    local_lists = draw_local_lists(jax.random.fold_in(key_of[5], 71), 0)
    remote_lists = draw_remote_lists(jax.random.fold_in(key_of[5], 71), 0)
    send_blocks = with_ends(jax.random.randint(key_of[4], (N_GROUP, N_GROUP), 0, GB), jax.random.fold_in(key_of[4], 1), 0, GB - 1).astype(jnp.int32)
    return dict(queries=queries, keys_values=keys_values, local_lists=local_lists, remote_lists=remote_lists, send_blocks=send_blocks)


def block_scores(query_heads, key_block):
    key_heads = key_block[:, :KV_HEADS * HEAD_DIM].reshape(BLOCK, KV_HEADS, HEAD_DIM)
    products = jnp.einsum("qgrd,kgd->qgrk", query_heads.astype(jnp.float32), key_heads.astype(jnp.float32))
    return products * (HEAD_DIM ** -0.5)


def block_mix(weight_block, key_block):
    value_heads = key_block[:, KV_HEADS * HEAD_DIM:].reshape(BLOCK, KV_HEADS, HEAD_DIM)
    return jnp.einsum("qgrk,kgd->qgrd", weight_block.astype(jnp.float32), value_heads.astype(jnp.float32))


def one_block(index, queries, keys_values, local_lists, remote_lists, send_blocks):
    repeat = HEADS // KV_HEADS
    group_index = index // GB
    local_row = local_lists[index]
    remote_row = remote_lists[index]
    source = jnp.maximum(remote_row, 0).astype(jnp.int32)
    chosen = jnp.concatenate([
        (group_index * GB + jnp.maximum(local_row, 0)).astype(jnp.int32),
        (source * GB + send_blocks[source, group_index]).astype(jnp.int32)]).astype(jnp.int32)
    usable = jnp.concatenate([local_row >= 0, remote_row >= 0])
    query_rows = lax.dynamic_slice_in_dim(queries, (index * BLOCK).astype(jnp.int32), BLOCK, 0)
    query_heads = query_rows.reshape(BLOCK, KV_HEADS, repeat, HEAD_DIM)
    empty_scores = jnp.zeros((BLOCK, KV_HEADS, repeat, BLOCK), jnp.float32)
    empty_mix = jnp.zeros((BLOCK, KV_HEADS, repeat, HEAD_DIM), jnp.float32)

    def score_slot(pair):
        block_id, keep = pair
        return lax.cond(keep, lambda: block_scores(query_heads, keys_values[block_id]), lambda: empty_scores)

    scores = lax.map(score_slot, (chosen, usable))
    scores = jnp.where(usable[:, None, None, None, None], scores, -jnp.inf)
    maxima = jnp.max(scores, axis=(0, 4), keepdims=True)
    weights = jnp.exp(scores - maxima)
    totals = jnp.sum(weights, axis=(0, 4))
    rounded = lax.optimization_barrier(weights.astype(jnp.bfloat16))

    def mix_slot(triple):
        block_id, keep, weight_block = triple
        return lax.cond(keep, lambda: block_mix(weight_block, keys_values[block_id]), lambda: empty_mix)

    blended = jnp.sum(lax.map(mix_slot, (chosen, usable, rounded)), axis=0)
    result = blended / totals[..., None]
    return result.reshape(BLOCK, HEADS * HEAD_DIM).astype(jnp.bfloat16)


def reference(queries, keys_values, local_lists, remote_lists, send_blocks):
    indices = jnp.arange(Q_BLOCKS, dtype=jnp.int32)
    blocks = lax.map(lambda index: one_block(index, queries, keys_values, local_lists, remote_lists, send_blocks), indices)
    return blocks.reshape(TOKENS, HEADS * HEAD_DIM)
```

```python
import functools

import jax
import jax.numpy as jnp
from jax import lax
from jax.experimental import pallas as pl
from jax.experimental.pallas import tpu as pltpu
from jax.sharding import PartitionSpec as P

HEADS, KV_HEADS, HEAD_DIM = 48, 8, 128
CH = 6
REPEAT = HEADS // KV_HEADS
SCALE = HEAD_DIM ** -0.5 * 1.4426950408889634


def attend_kernel(local_ref, remote_ref, table_ref, q_ref, pool_a, pool_b, out_ref, kv, stacked, scores, weights, sems):
    block, head = pl.program_id(0), pl.program_id(1)
    n_local, n_remote = local_ref.shape[1], remote_ref.shape[1]
    rows = q_ref.shape[0]
    keys = kv.shape[1] // (n_local + n_remote)
    members = keys // 8

    def counts(b):
        near = sum((local_ref[b, i] >= 0).astype(jnp.int32) for i in range(n_local))
        far = sum((remote_ref[b, i] >= 0).astype(jnp.int32) for i in range(n_remote))
        return near, far

    near, far = counts(block)
    total = near + far
    pairs = lax.div(total + 1, 2)

    def copy(b, pool, unit, slot, m):
        return pltpu.make_async_copy(
            pool.at[unit], kv.at[b, pl.ds(pl.multiple_of(slot * keys + m * 8, 8), 8), :], sems.at[b])

    def fetch(b):
        near, far = counts(b)

        def local_slot(s, _):
            which = local_ref[b, s]
            for m in range(members):
                copy(b, pool_a, table_ref[which * members + m], s, m).start()
            return 0

        def remote_slot(s, _):
            which = remote_ref[b, s] + 32
            for m in range(members):
                copy(b, pool_b, table_ref[which * members + m], near + s, m).start()
            return 0

        lax.fori_loop(0, near, local_slot, 0)
        lax.fori_loop(0, far, remote_slot, 0)

        @pl.when(lax.rem(near + far, 2) == 1)
        def _():
            which = local_ref[b, 0]
            for m in range(members):
                copy(b, pool_a, table_ref[which * members + m], near + far, m).start()

    @pl.when(jnp.logical_and(block == 0, head == 0))
    def _():
        for b in range(2):
            fetch(b)

    @pl.when(head == 0)
    def _():
        def drain(s, _):
            pltpu.make_async_copy(
                kv.at[block, pl.ds(0, 2 * keys), :], kv.at[block, pl.ds(0, 2 * keys), :], sems.at[block]).wait()
            return 0
        lax.fori_loop(0, pairs, drain, 0)

    kcol = pl.multiple_of(head * HEAD_DIM, HEAD_DIM)
    vcol = pl.multiple_of(KV_HEADS * HEAD_DIM + head * HEAD_DIM, HEAD_DIM)
    def work(pairs):
        for r in range(REPEAT):
            stacked[r * rows:(r + 1) * rows, :] = q_ref[:, r * HEAD_DIM:(r + 1) * HEAD_DIM]
        bias = jnp.where(2 * pairs == total, 0.0, -jnp.inf)
        q = stacked[...]
        for j in range(pairs):
            k = kv[block, j * 2 * keys:(j + 1) * 2 * keys, pl.ds(kcol, HEAD_DIM)]
            scores[j] = lax.dot_general(q, k, (((1,), (1,)), ((), ())), preferred_element_type=jnp.float32)
        for r in range(REPEAT):
            span = slice(r * rows, (r + 1) * rows)
            parts = []
            for j in range(pairs):
                parts.append(scores[j, span, :keys])
                last = scores[j, span, keys:]
                parts.append(last + bias if j == pairs - 1 else last)
            top = functools.reduce(jnp.maximum, parts)
            top = jnp.max(top, axis=1, keepdims=True) * SCALE
            for i, part in enumerate(parts):
                weights[span, i * keys:(i + 1) * keys] = jnp.exp2(part * SCALE - top).astype(jnp.bfloat16)
        v = kv[block, :pairs * 2 * keys, pl.ds(vcol, HEAD_DIM)]
        both = jnp.concatenate([v, jnp.ones((pairs * 2 * keys, HEAD_DIM), jnp.bfloat16)], axis=1)
        for r in range(0, REPEAT, CH):
            acc = jnp.dot(weights[r * rows:(r + CH) * rows, :pairs * 2 * keys], both, preferred_element_type=jnp.float32)
            out = (acc[:, :HEAD_DIM] / acc[:, HEAD_DIM:]).astype(jnp.bfloat16)
            for i in range(CH):
                out_ref[:, (r + i) * HEAD_DIM:(r + i + 1) * HEAD_DIM] = out[i * rows:(i + 1) * rows]

    for count in range(1, kv.shape[1] // (2 * keys) + 1):
        pl.when(pairs == count)(functools.partial(work, count))


def attend(local_lists, remote_lists, table, queries, pool_a, pool_b):
    blocks = local_lists.shape[0]
    rows = queries.shape[0] // blocks
    slots = local_lists.shape[1] + remote_lists.shape[1]
    keys = 128
    width = REPEAT * HEAD_DIM
    return pl.pallas_call(
        attend_kernel,
        out_shape=jax.ShapeDtypeStruct(queries.shape, jnp.bfloat16),
        grid_spec=pltpu.PrefetchScalarGridSpec(
            num_scalar_prefetch=3, grid=(blocks, KV_HEADS),
            in_specs=[pl.BlockSpec((rows, width), lambda b, h, *_: (b, h)),
                      pl.BlockSpec(memory_space=pl.ANY), pl.BlockSpec(memory_space=pl.ANY)],
            out_specs=pl.BlockSpec((rows, width), lambda b, h, *_: (b, h)),
            scratch_shapes=[
                pltpu.VMEM((blocks, slots * keys, 2 * KV_HEADS * HEAD_DIM), jnp.bfloat16),
                pltpu.VMEM((REPEAT * rows, HEAD_DIM), jnp.bfloat16),
                pltpu.VMEM((slots // 2, REPEAT * rows, 2 * keys), jnp.float32),
                pltpu.VMEM((REPEAT * rows, slots * keys), jnp.bfloat16),
                pltpu.SemaphoreType.DMA((blocks,)),
            ]),
        compiler_params=pltpu.CompilerParams(vmem_limit_bytes=56 << 20),
        name="attend",
    )(local_lists, remote_lists, table, queries, pool_a, pool_b)


def shards(queries, keys_values, local_lists, remote_lists, send_blocks):
    outgoing = jnp.take(keys_values, send_blocks[0], axis=0)
    arrived = lax.all_to_all(outgoing, "group", split_axis=0, concat_axis=0, tiled=True)
    near = lax.all_gather(keys_values, "member", axis=0, tiled=True)
    far = lax.all_gather(arrived, "member", axis=0, tiled=True)
    blocks, slabs = keys_values.shape[0], arrived.shape[0]
    members = near.shape[0] // blocks
    order = jnp.arange(members, dtype=jnp.int32)
    table = jnp.concatenate([
        (jnp.arange(blocks, dtype=jnp.int32)[:, None] + order * blocks).reshape(-1),
        (jnp.arange(slabs, dtype=jnp.int32)[:, None] + order * slabs).reshape(-1)])
    return attend(local_lists, remote_lists, table, queries, near, far)


def solution(mesh):
    placed = (
        P(("group", "member"), None),
        P("group", "member", None),
        P(("group", "member"), None),
        P(("group", "member"), None),
        P("group", None),
    )
    return jax.shard_map(
        shards, mesh=mesh, in_specs=placed, out_specs=P(("group", "member"), None), check_vma=False
    )
```

```python
import functools

import jax
import jax.numpy as jnp
from jax import lax
from jax.experimental import pallas as pl
from jax.experimental.pallas import tpu as pltpu
from jax.sharding import PartitionSpec as P

MESH = pl.DeviceIdType.MESH
HEADS, KV_HEADS, HEAD_DIM = 48, 8, 128
CH = 6
REPEAT = HEADS // KV_HEADS
SCALE = HEAD_DIM ** -0.5 * 1.4426950408889634


def attend_kernel(local_ref, remote_ref, table_ref, q_ref, pool, out_ref, kv, stacked, scores, weights, sems):
    block, head = pl.program_id(0), pl.program_id(1)
    n_local, n_remote = local_ref.shape[1], remote_ref.shape[1]
    rows = q_ref.shape[0]
    keys = kv.shape[1] // (n_local + n_remote)
    members = keys // 8

    def counts(b):
        near = sum((local_ref[b, i] >= 0).astype(jnp.int32) for i in range(n_local))
        far = sum((remote_ref[b, i] >= 0).astype(jnp.int32) for i in range(n_remote))
        return near, far

    near, far = counts(block)
    total = near + far
    pairs = lax.div(total + 1, 2)

    def copy(b, unit, slot, m):
        return pltpu.make_async_copy(
            pool.at[unit], kv.at[b, pl.ds(pl.multiple_of(slot * keys + m * 8, 8), 8), :], sems.at[b])

    def fetch(b):
        near, far = counts(b)

        def local_slot(s, _):
            which = local_ref[b, s]
            for m in range(members):
                copy(b, table_ref[m, which], s, m).start()
            return 0

        def remote_slot(s, _):
            which = remote_ref[b, s] + 32
            for m in range(members):
                copy(b, table_ref[m, which], near + s, m).start()
            return 0

        lax.fori_loop(0, near, local_slot, 0)
        lax.fori_loop(0, far, remote_slot, 0)

        @pl.when(lax.rem(near + far, 2) == 1)
        def _():
            which = local_ref[b, 0]
            for m in range(members):
                copy(b, table_ref[m, which], near + far, m).start()

    @pl.when(jnp.logical_and(block == 0, head == 0))
    def _():
        for b in range(2):
            fetch(b)

    @pl.when(head == 0)
    def _():
        def drain(s, _):
            pltpu.make_async_copy(
                kv.at[block, pl.ds(0, 2 * keys), :], kv.at[block, pl.ds(0, 2 * keys), :], sems.at[block]).wait()
            return 0
        lax.fori_loop(0, pairs, drain, 0)

    kcol = pl.multiple_of(head * HEAD_DIM, HEAD_DIM)
    vcol = pl.multiple_of(KV_HEADS * HEAD_DIM + head * HEAD_DIM, HEAD_DIM)
    def work(pairs):
        for r in range(REPEAT):
            stacked[r * rows:(r + 1) * rows, :] = q_ref[:, r * HEAD_DIM:(r + 1) * HEAD_DIM]
        bias = jnp.where(2 * pairs == total, 0.0, -jnp.inf)
        q = stacked[...]
        for j in range(pairs):
            k = kv[block, j * 2 * keys:(j + 1) * 2 * keys, pl.ds(kcol, HEAD_DIM)]
            scores[j] = lax.dot_general(q, k, (((1,), (1,)), ((), ())), preferred_element_type=jnp.float32)
        for r in range(REPEAT):
            span = slice(r * rows, (r + 1) * rows)
            parts = []
            for j in range(pairs):
                parts.append(scores[j, span, :keys])
                last = scores[j, span, keys:]
                parts.append(last + bias if j == pairs - 1 else last)
            top = functools.reduce(jnp.maximum, parts)
            top = jnp.max(top, axis=1, keepdims=True) * SCALE
            for i, part in enumerate(parts):
                weights[span, i * keys:(i + 1) * keys] = jnp.exp2(part * SCALE - top).astype(jnp.bfloat16)
        v = kv[block, :pairs * 2 * keys, pl.ds(vcol, HEAD_DIM)]
        both = jnp.concatenate([v, jnp.ones((pairs * 2 * keys, HEAD_DIM), jnp.bfloat16)], axis=1)
        for r in range(0, REPEAT, CH):
            acc = jnp.dot(weights[r * rows:(r + CH) * rows, :pairs * 2 * keys], both, preferred_element_type=jnp.float32)
            out = (acc[:, :HEAD_DIM] / acc[:, HEAD_DIM:]).astype(jnp.bfloat16)
            for i in range(CH):
                out_ref[:, (r + i) * HEAD_DIM:(r + i + 1) * HEAD_DIM] = out[i * rows:(i + 1) * rows]

    for count in range(1, kv.shape[1] // (2 * keys) + 1):
        pl.when(pairs == count)(functools.partial(work, count))


def attend(local_lists, remote_lists, table, queries, pool):
    blocks = local_lists.shape[0]
    rows = queries.shape[0] // blocks
    slots = local_lists.shape[1] + remote_lists.shape[1]
    keys = 128
    width = REPEAT * HEAD_DIM
    return pl.pallas_call(
        attend_kernel,
        out_shape=jax.ShapeDtypeStruct(queries.shape, jnp.bfloat16),
        grid_spec=pltpu.PrefetchScalarGridSpec(
            num_scalar_prefetch=3, grid=(blocks, KV_HEADS),
            in_specs=[pl.BlockSpec((rows, width), lambda b, h, *_: (b, h)),
                      pl.BlockSpec(memory_space=pl.ANY)],
            out_specs=pl.BlockSpec((rows, width), lambda b, h, *_: (b, h)),
            scratch_shapes=[
                pltpu.VMEM((blocks, slots * keys, 2 * KV_HEADS * HEAD_DIM), jnp.bfloat16),
                pltpu.VMEM((REPEAT * rows, HEAD_DIM), jnp.bfloat16),
                pltpu.VMEM((slots // 2, REPEAT * rows, 2 * keys), jnp.float32),
                pltpu.VMEM((REPEAT * rows, slots * keys), jnp.bfloat16),
                pltpu.SemaphoreType.DMA((blocks,)),
            ]),
        compiler_params=pltpu.CompilerParams(vmem_limit_bytes=56 << 20),
        name="attend",
    )(local_lists, remote_lists, table, queries, pool)


def spread_kernel(caps, kv_hbm, entries, targets, pool, table, full_flag, kvv, comb, outgoing, lists, need, route, route_s,
                  over, overs, sent, got, own_s, own_r, cast_s, cast_r, list_s, list_r, over_s, over_r, ring_s, ring_r,
                  twin_s, twin_r, near):
    g, m = lax.axis_index("group"), lax.axis_index("member")
    groups, members, depth = comb.shape[0] - kvv.shape[0], lists.shape[0] * 2, len(caps)
    blocks, chips = kvv.shape[0], lists.shape[0]
    held = blocks + groups
    own_blocks = blocks // members
    z, c = m // 2, m % 2
    twin = z * 2 + (1 - c)
    total = sum(caps)
    twin_at, own_at, own_twin_at = held, 2 * held, 2 * held + blocks
    ring_at = 2 * held + 2 * blocks
    ring_twin_at = ring_at + 2 * total

    def offset(way, step):
        return way * total + sum(caps[:step])

    loads = [pltpu.make_async_copy(kv_hbm, kvv, near.at[0]),
             pltpu.make_async_copy(kv_hbm, comb.at[pl.ds(0, blocks)], near.at[1]),
             pltpu.make_async_copy(entries, lists.at[0, c], near.at[2])]
    for load in loads:
        load.start()

    barrier = pltpu.get_barrier_semaphore()

    def greet(k, _):
        pl.semaphore_signal(barrier, inc=1, device_id={"member": (m + k) % members}, device_id_type=MESH)
        return 0

    def greet_group(k, _):
        pl.semaphore_signal(barrier, inc=1, device_id={"group": (g + k) % groups}, device_id_type=MESH)
        return 0

    lax.fori_loop(1, members, greet, 0)
    lax.fori_loop(1, groups, greet_group, 0)
    pl.semaphore_wait(barrier, members + groups - 2)

    def list_copy(k):
        to = (m + k) % members
        slot = (z - to // 2 + chips) % chips
        return pltpu.make_async_remote_copy(
            src_ref=entries, dst_ref=lists.at[slot, c], send_sem=list_s.at[k], recv_sem=list_r.at[slot * 2 + c],
            device_id={"member": to}, device_id_type=MESH)

    def list_start(k, _):
        list_copy(k).start()
        return 0

    lax.fori_loop(1, members, list_start, 0)

    loads[0].wait()

    def pick(i, _):
        outgoing[i] = kvv[targets[0, i]]
        return 0

    lax.fori_loop(0, groups, pick, 0)

    def cast_copy(k):
        to = (g + k) % groups
        return pltpu.make_async_remote_copy(
            src_ref=outgoing.at[to], dst_ref=comb.at[blocks + g], send_sem=cast_s.at[k], recv_sem=cast_r.at[g],
            device_id={"group": to}, device_id_type=MESH)

    def cast_start(k, _):
        cast_copy(k).start()
        return 0

    lax.fori_loop(1, groups, cast_start, 0)
    loads.append(pltpu.make_async_copy(outgoing.at[g], comb.at[blocks + g], near.at[3]))
    loads[3].start()

    def own_copy(to):
        return pltpu.make_async_remote_copy(
            src_ref=kv_hbm.at[pl.ds(to * own_blocks, own_blocks)],
            dst_ref=pool.at[pl.ds(own_at + m * own_blocks, own_blocks)],
            send_sem=own_s.at[to], recv_sem=own_r.at[m], device_id={"member": to}, device_id_type=MESH)

    def own_start(*shifts):
        for shift in shifts:
            for core in range(2):
                own_copy((z + shift) % chips * 2 + core).start()

    own_start(3, chips - 3)
    keep = pltpu.make_async_copy(kvv.at[pl.ds(m * own_blocks, own_blocks)],
                                 pool.at[pl.ds(own_at + m * own_blocks, own_blocks)], near.at[4])
    keep.start()

    def list_wait(k, _):
        frm = (m + k) % members
        slot = (frm // 2 - z + chips) % chips
        pltpu.make_async_remote_copy(
            src_ref=entries, dst_ref=lists.at[slot, frm % 2], send_sem=list_s.at[k],
            recv_sem=list_r.at[slot * 2 + frm % 2], device_id={"member": frm}, device_id_type=MESH).wait_recv()
        return 0

    loads[2].wait()
    lax.fori_loop(1, members, list_wait, 0)
    lane = lax.broadcasted_iota(jnp.int32, (16, 128), 1)
    for k in range(chips):
        found = jnp.maximum(jnp.where(lists[k, 0] == lane, 1.0, 0.0), jnp.where(lists[k, 1] == lane, 1.0, 0.0))
        need[k:k + 1, :] = jnp.max(found, axis=0, keepdims=True)
    lane = lax.broadcasted_iota(jnp.int32, (chips, 128), 1)
    chip = (lax.broadcasted_iota(jnp.int32, (chips, 128), 0) + z) % chips
    own_width = 2 * own_blocks
    mine = jnp.logical_and(lane >= chip * own_width, lane < chip * own_width + own_width)
    wanted = jnp.where(mine, 0.0, need[...])
    even = jnp.where(lane % 2 == 0, 1.0, 0.0)
    wants = []
    for way in range(2):
        ahead = [pltpu.roll(wanted, (chips - d if way == 0 else d) % chips, 0) for d in range(depth + 1)]
        half = even if way == 0 else 1.0 - even
        for step in range(depth):
            far = depth - step
            flags = ahead[far] * half
            for k in range(1, far):
                flags = jnp.maximum(flags, ahead[k])
            wants.append(flags)
    lower = jnp.where(lax.broadcasted_iota(jnp.int32, (128, 128), 0) < lax.broadcasted_iota(jnp.int32, (128, 128), 1), 1.0, 0.0)
    stacked = jnp.concatenate(wants, axis=0)
    places = jnp.dot(stacked.astype(jnp.bfloat16), lower.astype(jnp.bfloat16), preferred_element_type=jnp.float32)
    places = [places[i * chips:(i + 1) * chips] for i in range(2 * depth)]
    lane_row = lax.broadcasted_iota(jnp.int32, (1, 128), 1)
    slot_ids = lax.broadcasted_iota(jnp.int32, route.shape, 0).astype(jnp.float32)
    columns = lax.broadcasted_iota(jnp.int32, route.shape, 1)
    picks = jnp.zeros(route.shape, jnp.float32)
    too_many = jnp.zeros((chips, 1), jnp.float32)
    for way in range(2):
        source = chips - 1 if way == 0 else 1
        for step in range(depth):
            i = way * depth + step
            flags, place = wants[i][0:1], places[i][0:1]
            value = lane_row.astype(jnp.float32) if step == 0 else places[i - 1][source:source + 1]
            hit = jnp.where(place == slot_ids, flags * value, 0.0)
            picks = jnp.where(columns == i, jnp.sum(hit, axis=1, keepdims=True), picks)
            count = jnp.sum(wants[i], axis=1, keepdims=True)
            too_many = jnp.maximum(too_many, jnp.where(count > caps[step], 1.0, 0.0))
    route[...] = picks.astype(jnp.int32)
    to_smem = pltpu.make_async_copy(route, route_s, near.at[5])
    to_smem.start()
    over[...] = jnp.broadcast_to(jnp.max(too_many, axis=0, keepdims=True), over.shape).astype(jnp.int32)

    core_block = lane_row // own_blocks
    for k in range(chips):
        zz = (z + k) % chips
        for t in range(2):
            if k == 0:
                row = lane_row + t * twin_at
            else:
                base = ring_at if t == 0 else ring_twin_at
                plus = places[min(chips - k, depth) - 1][chips - 1:chips].astype(jnp.int32) + base + offset(0, min(chips - k, depth) - 1)
                minus = places[depth + min(k, depth) - 1][1:2].astype(jnp.int32) + base + offset(1, min(k, depth) - 1)
                if k < depth:
                    row = minus
                elif k > depth:
                    row = plus
                else:
                    row = jnp.where(lane_row % 2 == 0, plus, minus)
                member = zz * 2 + (c if t == 0 else 1 - c)
                row = jnp.where(core_block == m, own_at + member * own_blocks + lane_row - m * own_blocks, row)
                row = jnp.where(core_block == twin, own_twin_at + member * own_blocks + lane_row - twin * own_blocks, row)
            table[2 * k + t:2 * k + t + 1, :] = row

    loads[1].wait()
    loads[3].wait()

    def cast_wait(k, _):
        frm = (g + k) % groups
        pltpu.make_async_remote_copy(
            src_ref=outgoing.at[frm], dst_ref=comb.at[blocks + frm], send_sem=cast_s.at[k], recv_sem=cast_r.at[frm],
            device_id={"group": frm}, device_id_type=MESH).wait_recv()
        return 0

    lax.fori_loop(1, groups, cast_wait, 0)
    to_smem.wait()
    keeps = [keep, pltpu.make_async_copy(comb, pool.at[pl.ds(0, held)], near.at[6])]
    keeps[1].start()
    twins = [pltpu.make_async_remote_copy(
        src_ref=comb, dst_ref=pool.at[pl.ds(twin_at, held)], send_sem=twin_s.at[0], recv_sem=twin_r.at[0],
        device_id={"member": twin}, device_id_type=MESH)]

    def ring(way, step):
        at = offset(way, step)
        to = (m + 2) % members if way == 0 else (m + members - 2) % members
        return pltpu.make_async_remote_copy(
            src_ref=sent[way * depth + step], dst_ref=got[way * depth + step],
            send_sem=ring_s.at[way * depth + step], recv_sem=ring_r.at[way * depth + step],
            device_id={"member": to}, device_id_type=MESH)

    def pack(way, step):
        i = way * depth + step
        source, target = (comb if step == 0 else got[i - 1]), sent[i]

        def one(j, _):
            target[j] = source[jnp.clip(route_s[j, i], 0, source.shape[0] - 1)]
            return 0

        lax.fori_loop(0, caps[step], one, 0)
        ring(way, step).start()

    later = [(depth,), (2, chips - 2), (1, chips - 1), ()]

    def over_copy(k):
        to = (g + k) % groups
        return pltpu.make_async_remote_copy(
            src_ref=over, dst_ref=overs.at[g], send_sem=over_s.at[k], recv_sem=over_r.at[g],
            device_id={"group": to}, device_id_type=MESH)

    for step in range(depth):
        for way in range(2):
            i = way * depth + step
            if step > 0:
                ring(way, step - 1).wait_recv()
            pack(way, step)
            if step > 0:
                at, size = offset(way, step - 1), caps[step - 1]
                twins.append(pltpu.make_async_remote_copy(
                    src_ref=got[i - 1], dst_ref=pool.at[pl.ds(ring_twin_at + at, size)],
                    send_sem=twin_s.at[2 + i - 1], recv_sem=twin_r.at[2 + i - 1], device_id={"member": twin}, device_id_type=MESH))
                twins[-1].start()
                keeps.append(pltpu.make_async_copy(got[i - 1], pool.at[pl.ds(ring_at + at, size)], near.at[8 + i - 1]))
                keeps[-1].start()
        own_start(*later[step])
        if step == 0:
            twins[0].start()

            def over_start(k, _):
                over_copy(k).start()
                return 0

            lax.fori_loop(1, groups, over_start, 0)
            alone = pltpu.make_async_copy(over, overs.at[g], near.at[7])
            alone.start()
            own_copy(twin).start()

    def own_wait(k, _):
        frm = (m + k) % members
        pltpu.make_async_remote_copy(
            src_ref=kv_hbm.at[pl.ds(0, own_blocks)], dst_ref=pool.at[pl.ds(own_at + frm * own_blocks, own_blocks)],
            send_sem=own_s.at[frm], recv_sem=own_r.at[frm], device_id={"member": frm}, device_id_type=MESH).wait_recv()
        return 0

    lax.fori_loop(1, members, own_wait, 0)
    keep.wait()
    twins.append(pltpu.make_async_remote_copy(
        src_ref=pool.at[pl.ds(own_at, blocks)], dst_ref=pool.at[pl.ds(own_twin_at, blocks)],
        send_sem=twin_s.at[1], recv_sem=twin_r.at[1], device_id={"member": twin}, device_id_type=MESH))
    twins[-1].start()

    def over_wait(k, _):
        frm = (g + k) % groups
        pltpu.make_async_remote_copy(
            src_ref=over, dst_ref=overs.at[frm], send_sem=over_s.at[k], recv_sem=over_r.at[frm],
            device_id={"group": frm}, device_id_type=MESH).wait_recv()
        return 0

    lax.fori_loop(1, groups, over_wait, 0)
    alone.wait()
    full_flag[...] = jnp.max(overs[...], axis=0)

    for way in range(2):
        i = way * depth + depth - 1
        at, size = offset(way, depth - 1), caps[depth - 1]
        ring(way, depth - 1).wait_recv()
        twins.append(pltpu.make_async_remote_copy(
            src_ref=got[i], dst_ref=pool.at[pl.ds(ring_twin_at + at, size)],
            send_sem=twin_s.at[2 + i], recv_sem=twin_r.at[2 + i], device_id={"member": twin}, device_id_type=MESH))
        twins[-1].start()
        keeps.append(pltpu.make_async_copy(got[i], pool.at[pl.ds(ring_at + at, size)], near.at[8 + i]))
        keeps[-1].start()

    def drain(k, _):
        list_copy(k).wait_send()
        own_copy((m + k) % members).wait_send()
        return 0

    def drain_group(k, _):
        cast_copy(k).wait_send()
        over_copy(k).wait_send()
        return 0

    lax.fori_loop(1, members, drain, 0)
    lax.fori_loop(1, groups, drain_group, 0)
    for way in range(2):
        for step in range(depth):
            ring(way, step).wait_send()
    for copy in twins:
        copy.wait()
    for copy in keeps[1:]:
        copy.wait()


def spread(caps, collective_id, keys_values, entries, targets):
    blocks, share, width = keys_values.shape
    groups, members = targets.shape[1], 16
    chips, depth = members // 2, len(caps)
    held, total = blocks + groups, sum(caps)
    units = 2 * held + 2 * blocks + 4 * total
    unit = (share, width)
    dma = pltpu.SemaphoreType.DMA
    rings = [pltpu.VMEM((cap,) + unit, jnp.bfloat16) for _ in range(2) for cap in caps]
    depth_pad = -(-max(caps) // 8) * 8

    def kernel(*refs):
        lead, rings_at = 15, 15 + 2 * depth
        spread_kernel(caps, *refs[:lead], refs[lead:rings_at], refs[rings_at:rings_at + 2 * depth], *refs[rings_at + 2 * depth:])

    return pl.pallas_call(
        kernel,
        out_shape=(jax.ShapeDtypeStruct((units,) + unit, jnp.bfloat16),
                   jax.ShapeDtypeStruct((members, 128), jnp.int32),
                   jax.ShapeDtypeStruct((8, 128), jnp.int32)),
        in_specs=[pl.BlockSpec(memory_space=pl.ANY), pl.BlockSpec(memory_space=pltpu.VMEM),
                  pl.BlockSpec(memory_space=pltpu.SMEM)],
        out_specs=(pl.BlockSpec(memory_space=pl.ANY), pl.BlockSpec(memory_space=pltpu.VMEM),
                   pl.BlockSpec(memory_space=pltpu.VMEM)),
        scratch_shapes=[
            pltpu.VMEM((blocks,) + unit, jnp.bfloat16),
            pltpu.VMEM((held,) + unit, jnp.bfloat16),
            pltpu.VMEM((groups,) + unit, jnp.bfloat16),
            pltpu.VMEM((chips, 2, 16, 128), jnp.int32),
            pltpu.VMEM((chips, 128), jnp.float32),
            pltpu.VMEM((depth_pad, 128), jnp.int32),
            pltpu.SMEM((depth_pad, 128), jnp.int32),
            pltpu.VMEM((8, 128), jnp.int32),
            pltpu.VMEM((groups, 8, 128), jnp.int32),
        ] + rings + rings + [
            dma((members,)), dma((members,)), dma((groups,)), dma((groups,)), dma((members,)), dma((members,)),
            dma((groups,)), dma((groups,)), dma((2 * depth,)), dma((2 * depth,)), dma((2 + 2 * depth,)), dma((2 + 2 * depth,)),
            dma((8 + 2 * depth,)),
        ],
        compiler_params=pltpu.CompilerParams(
            collective_id=collective_id, has_side_effects=True, vmem_limit_bytes=60 << 20),
        name="spread",
    )(keys_values, entries, targets)


FEW = (31, 27, 21, 11)


def shards(queries, keys_values, local_lists, remote_lists, send_blocks):
    blocks, groups = keys_values.shape[0], send_blocks.shape[1]
    entries = jnp.concatenate([
        local_lists.reshape(-1), jnp.where(remote_lists >= 0, remote_lists + blocks, -1).reshape(-1)])
    entries = jnp.broadcast_to(entries[:, None], (entries.shape[0], 128))
    pool, table, over = spread(FEW, 0, keys_values, entries, send_blocks)

    def enough():
        return attend(local_lists, remote_lists, table, queries, pool)

    def whole():
        held = blocks + groups
        pool, table, _ = spread((held, held, held, held // 2), 1, keys_values, entries, send_blocks)
        return attend(local_lists, remote_lists, table, queries, pool)

    return lax.cond(over[0, 0] > 0, whole, enough)


def solution(mesh):
    placed = (
        P(("group", "member"), None),
        P("group", "member", None),
        P(("group", "member"), None),
        P(("group", "member"), None),
        P("group", None),
    )
    return jax.shard_map(
        shards, mesh=mesh, in_specs=placed, out_specs=P(("group", "member"), None), check_vma=False
    )
```

```python
import functools

import jax
import jax.numpy as jnp
from jax import lax
from jax.experimental import pallas as pl
from jax.experimental.pallas import tpu as pltpu
from jax.sharding import PartitionSpec as P

MESH = pl.DeviceIdType.MESH
HEADS, KV_HEADS, HEAD_DIM = 48, 8, 128
CH = 6
REPEAT = HEADS // KV_HEADS
SCALE = HEAD_DIM ** -0.5 * 1.4426950408889634


def attend_kernel(local_ref, remote_ref, table_ref, q_ref, pool, out_ref, kv, scores_a, scores_b, weights_a, weights_b, sems):
    scores, weights = (scores_a, scores_b), (weights_a, weights_b)
    block = pl.program_id(0)
    n_local, n_remote = local_ref.shape[1], remote_ref.shape[1]
    rows = q_ref.shape[0]
    keys = kv.shape[1] // (n_local + n_remote)
    members = keys // 8

    def counts(b):
        near = sum((local_ref[b, i] >= 0).astype(jnp.int32) for i in range(n_local))
        far = sum((remote_ref[b, i] >= 0).astype(jnp.int32) for i in range(n_remote))
        return near, far

    near, far = counts(block)
    total = near + far
    pairs = lax.div(total + 1, 2)

    def fetch(b):
        near, far = counts(b)
        total = near + far
        last = total + lax.rem(total, 2)

        def slot_copies(s, _):
            part = jnp.where(s < near, local_ref[b, jnp.minimum(s, n_local - 1)],
                             remote_ref[b, jnp.clip(s - near, 0, n_remote - 1)] + 32)
            which = jnp.where(s < total, part, local_ref[b, 0])
            for m in range(members):
                pltpu.make_async_copy(
                    pool.at[table_ref[m, which]],
                    kv.at[b, pl.ds(pl.multiple_of(s * keys + m * 8, 8), 8), :], sems.at[b]).start()
            return 0

        lax.fori_loop(0, last, slot_copies, 0)

    @pl.when(block == 0)
    def _():
        for b in range(kv.shape[0]):
            fetch(b)

    def drain(s, _):
        pltpu.make_async_copy(
            kv.at[block, pl.ds(0, 2 * keys), :], kv.at[block, pl.ds(0, 2 * keys), :], sems.at[block]).wait()
        return 0

    lax.fori_loop(0, pairs, drain, 0)

    share = REPEAT // 2

    def work(pairs):
        bias = jnp.where(2 * pairs == total, 0.0, -jnp.inf)

        def column(head, part, r):
            return pl.ds(pl.multiple_of((head * REPEAT + part * share + r) * HEAD_DIM, HEAD_DIM), HEAD_DIM)

        def score(head, part):
            q = jnp.concatenate([q_ref[:, column(head, part, r)] for r in range(share)], axis=0)
            for j in range(pairs):
                k = kv[block, j * 2 * keys:(j + 1) * 2 * keys, pl.ds(pl.multiple_of(head * HEAD_DIM, HEAD_DIM), HEAD_DIM)]
                scores[part][j] = lax.dot_general(q, k, (((1,), (1,)), ((), ())), preferred_element_type=jnp.float32)

        def weigh(part):
            for r in range(share):
                span = slice(r * rows, (r + 1) * rows)
                parts = []
                for j in range(pairs):
                    parts.append(scores[part][j, span, :keys])
                    last = scores[part][j, span, keys:]
                    parts.append(last + bias if j == pairs - 1 else last)
                top = functools.reduce(jnp.maximum, parts)
                top = jnp.max(top, axis=1, keepdims=True) * SCALE
                for i, piece in enumerate(parts):
                    weights[part][span, i * keys:(i + 1) * keys] = jnp.exp2(piece * SCALE - top).astype(jnp.bfloat16)

        def mix(head, part):
            at = pl.multiple_of((KV_HEADS + head) * HEAD_DIM, HEAD_DIM)
            v = kv[block, :pairs * 2 * keys, pl.ds(at, HEAD_DIM)]
            both = jnp.concatenate([v, jnp.ones((pairs * 2 * keys, HEAD_DIM), jnp.bfloat16)], axis=1)
            acc = jnp.concatenate([
                jnp.dot(weights[part][h:h + share * rows // 2, :pairs * 2 * keys], both, preferred_element_type=jnp.float32)
                for h in range(0, share * rows, share * rows // 2)], axis=0)
            out = (acc[:, :HEAD_DIM] / acc[:, HEAD_DIM:]).astype(jnp.bfloat16)
            for r in range(share):
                out_ref[:, column(head, part, r)] = out[r * rows:(r + 1) * rows]

        def step(head, _):
            score(head, 1)
            weigh(0)
            mix(jnp.maximum(head - 1, 0), 1)
            score(jnp.minimum(head + 1, KV_HEADS - 1), 0)
            weigh(1)
            mix(head, 0)
            return 0

        score(0, 0)
        lax.fori_loop(0, KV_HEADS, step, 0)
        mix(KV_HEADS - 1, 1)

    for count in range(1, kv.shape[1] // (2 * keys) + 1):
        pl.when(pairs == count)(functools.partial(work, count))


def attend(local_lists, remote_lists, table, queries, pool):
    blocks = local_lists.shape[0]
    rows = queries.shape[0] // blocks
    slots = local_lists.shape[1] + remote_lists.shape[1]
    keys = 128
    return pl.pallas_call(
        attend_kernel,
        out_shape=jax.ShapeDtypeStruct(queries.shape, jnp.bfloat16),
        grid_spec=pltpu.PrefetchScalarGridSpec(
            num_scalar_prefetch=3, grid=(blocks,),
            in_specs=[pl.BlockSpec((rows, queries.shape[1]), lambda b, *_: (b, 0)),
                      pl.BlockSpec(memory_space=pl.ANY)],
            out_specs=pl.BlockSpec((rows, queries.shape[1]), lambda b, *_: (b, 0)),
            scratch_shapes=[
                pltpu.VMEM((blocks, slots * keys, 2 * KV_HEADS * HEAD_DIM), jnp.bfloat16),
                pltpu.VMEM((slots // 2, REPEAT // 2 * rows, 2 * keys), jnp.float32),
                pltpu.VMEM((slots // 2, REPEAT // 2 * rows, 2 * keys), jnp.float32),
                pltpu.VMEM((REPEAT // 2 * rows, slots * keys), jnp.bfloat16),
                pltpu.VMEM((REPEAT // 2 * rows, slots * keys), jnp.bfloat16),
                pltpu.SemaphoreType.DMA((blocks,)),
            ]),
        compiler_params=pltpu.CompilerParams(
            vmem_limit_bytes=62 << 20),
        name="attend",
    )(local_lists, remote_lists, table, queries, pool)


def spread_kernel(caps, kv_hbm, local_ref, remote_ref, targets, pool, table, full_flag, entries, kvv, comb, outgoing, lists, need, route, route_s,
                  over, overs, sent, got, own_s, own_r, cast_s, cast_r, list_s, list_r, over_s, over_r, ring_s, ring_r,
                  twin_s, twin_r, near):
    g, m = lax.axis_index("group"), lax.axis_index("member")
    groups, members, depth = comb.shape[0] - kvv.shape[0], lists.shape[0] * 2, len(caps)
    blocks, chips = kvv.shape[0], lists.shape[0]
    held = blocks + groups
    own_blocks = blocks // members
    z, c = m // 2, m % 2
    twin = z * 2 + (1 - c)
    total = sum(caps)
    twin_at, own_at, own_twin_at = held, 2 * held, 2 * held + blocks
    ring_at = 2 * held + 2 * blocks
    ring_twin_at = ring_at + 2 * total

    def offset(way, step):
        return way * total + sum(caps[:step])

    n_local, n_remote = local_ref.shape[1], remote_ref.shape[1]
    for b in range(local_ref.shape[0]):
        for i in range(n_local):
            entries[b * n_local + i:b * n_local + i + 1, :] = jnp.full((1, 128), local_ref[b, i], jnp.int32)
        for i in range(n_remote):
            at = local_ref.shape[0] * n_local + b * n_remote + i
            other = remote_ref[b, i]
            entries[at:at + 1, :] = jnp.full((1, 128), jnp.where(other >= 0, other + blocks, -1), jnp.int32)

    loads = [pltpu.make_async_copy(kv_hbm, kvv, near.at[0]),
             pltpu.make_async_copy(kv_hbm, comb.at[pl.ds(0, blocks)], near.at[1]),
             pltpu.make_async_copy(entries, lists.at[0, c], near.at[2])]
    loads[0].start()
    loads[1].start()

    barrier = pltpu.get_barrier_semaphore()

    def greet(k, _):
        pl.semaphore_signal(barrier, inc=1, device_id={"member": (m + k) % members}, device_id_type=MESH)
        return 0

    def greet_group(k, _):
        pl.semaphore_signal(barrier, inc=1, device_id={"group": (g + k) % groups}, device_id_type=MESH)
        return 0

    lax.fori_loop(1, members, greet, 0)
    lax.fori_loop(1, groups, greet_group, 0)
    pl.semaphore_wait(barrier, members + groups - 2)

    def list_copy(k):
        to = (m + k) % members
        slot = (z - to // 2 + chips) % chips
        return pltpu.make_async_remote_copy(
            src_ref=entries, dst_ref=lists.at[slot, c], send_sem=list_s.at[k], recv_sem=list_r.at[slot * 2 + c],
            device_id={"member": to}, device_id_type=MESH)

    def list_start(k, _):
        list_copy(k).start()
        return 0

    loads[2].start()
    lax.fori_loop(1, members, list_start, 0)

    loads[0].wait()

    def pick(i, _):
        outgoing[i] = kvv[targets[0, i]]
        return 0

    lax.fori_loop(0, groups, pick, 0)

    def cast_copy(k):
        to = (g + k) % groups
        return pltpu.make_async_remote_copy(
            src_ref=outgoing.at[to], dst_ref=comb.at[blocks + g], send_sem=cast_s.at[k], recv_sem=cast_r.at[g],
            device_id={"group": to}, device_id_type=MESH)

    def cast_start(k, _):
        cast_copy(k).start()
        return 0

    lax.fori_loop(1, groups, cast_start, 0)
    loads.append(pltpu.make_async_copy(outgoing.at[g], comb.at[blocks + g], near.at[3]))
    loads[3].start()

    def own_copy(to):
        return pltpu.make_async_remote_copy(
            src_ref=kv_hbm.at[pl.ds(to * own_blocks, own_blocks)],
            dst_ref=pool.at[pl.ds(own_at + m * own_blocks, own_blocks)],
            send_sem=own_s.at[to], recv_sem=own_r.at[m], device_id={"member": to}, device_id_type=MESH)

    def own_start(*shifts):
        for shift in shifts:
            for core in range(2):
                own_copy((z + shift) % chips * 2 + core).start()

    own_start(3, chips - 3)
    keep = pltpu.make_async_copy(kvv.at[pl.ds(m * own_blocks, own_blocks)],
                                 pool.at[pl.ds(own_at + m * own_blocks, own_blocks)], near.at[4])
    keep.start()

    def list_wait(k, _):
        frm = (m + k) % members
        slot = (frm // 2 - z + chips) % chips
        pltpu.make_async_remote_copy(
            src_ref=entries, dst_ref=lists.at[slot, frm % 2], send_sem=list_s.at[k],
            recv_sem=list_r.at[slot * 2 + frm % 2], device_id={"member": frm}, device_id_type=MESH).wait_recv()
        return 0

    loads[2].wait()
    lax.fori_loop(1, members, list_wait, 0)
    lane = lax.broadcasted_iota(jnp.int32, (16, 128), 1)
    for k in range(chips):
        found = jnp.maximum(jnp.where(lists[k, 0] == lane, 1.0, 0.0), jnp.where(lists[k, 1] == lane, 1.0, 0.0))
        need[k:k + 1, :] = jnp.max(found, axis=0, keepdims=True)
    lane = lax.broadcasted_iota(jnp.int32, (chips, 128), 1)
    chip = (lax.broadcasted_iota(jnp.int32, (chips, 128), 0) + z) % chips
    own_width = 2 * own_blocks
    mine = jnp.logical_and(lane >= chip * own_width, lane < chip * own_width + own_width)
    wanted = jnp.where(mine, 0.0, need[...])
    even = jnp.where(lane % 2 == 0, 1.0, 0.0)
    wants = []
    for way in range(2):
        ahead = [pltpu.roll(wanted, (chips - d if way == 0 else d) % chips, 0) for d in range(depth + 1)]
        half = even if way == 0 else 1.0 - even
        for step in range(depth):
            far = depth - step
            flags = ahead[far] * half
            for k in range(1, far):
                flags = jnp.maximum(flags, ahead[k])
            wants.append(flags)
    lower = jnp.where(lax.broadcasted_iota(jnp.int32, (128, 128), 0) < lax.broadcasted_iota(jnp.int32, (128, 128), 1), 1.0, 0.0)
    stacked = jnp.concatenate(wants, axis=0)
    places = jnp.dot(stacked.astype(jnp.bfloat16), lower.astype(jnp.bfloat16), preferred_element_type=jnp.float32)
    places = [places[i * chips:(i + 1) * chips] for i in range(2 * depth)]
    lane_row = lax.broadcasted_iota(jnp.int32, (1, 128), 1)
    slot_ids = lax.broadcasted_iota(jnp.int32, route.shape, 0).astype(jnp.float32)
    columns = lax.broadcasted_iota(jnp.int32, route.shape, 1)
    picks = jnp.zeros(route.shape, jnp.float32)
    too_many = jnp.zeros((chips, 1), jnp.float32)
    for way in range(2):
        source = chips - 1 if way == 0 else 1
        for step in range(depth):
            i = way * depth + step
            flags, place = wants[i][0:1], places[i][0:1]
            value = lane_row.astype(jnp.float32) if step == 0 else places[i - 1][source:source + 1]
            hit = jnp.where(place == slot_ids, flags * value, 0.0)
            picks = jnp.where(columns == i, jnp.sum(hit, axis=1, keepdims=True), picks)
            count = jnp.sum(wants[i], axis=1, keepdims=True)
            too_many = jnp.maximum(too_many, jnp.where(count > caps[step], 1.0, 0.0))
    route[...] = picks.astype(jnp.int32)
    to_smem = pltpu.make_async_copy(route, route_s, near.at[5])
    to_smem.start()
    over[...] = jnp.broadcast_to(jnp.max(too_many, axis=0, keepdims=True), over.shape).astype(jnp.int32)

    core_block = lane_row // own_blocks
    for k in range(chips):
        zz = (z + k) % chips
        for t in range(2):
            if k == 0:
                row = lane_row + t * twin_at
            else:
                base = ring_at if t == 0 else ring_twin_at
                plus = places[min(chips - k, depth) - 1][chips - 1:chips].astype(jnp.int32) + base + offset(0, min(chips - k, depth) - 1)
                minus = places[depth + min(k, depth) - 1][1:2].astype(jnp.int32) + base + offset(1, min(k, depth) - 1)
                if k < depth:
                    row = minus
                elif k > depth:
                    row = plus
                else:
                    row = jnp.where(lane_row % 2 == 0, plus, minus)
                member = zz * 2 + (c if t == 0 else 1 - c)
                row = jnp.where(core_block == m, own_at + member * own_blocks + lane_row - m * own_blocks, row)
                row = jnp.where(core_block == twin, own_twin_at + member * own_blocks + lane_row - twin * own_blocks, row)
            table[2 * k + t:2 * k + t + 1, :] = row

    loads[1].wait()
    loads[3].wait()

    def cast_wait(k, _):
        frm = (g + k) % groups
        pltpu.make_async_remote_copy(
            src_ref=outgoing.at[frm], dst_ref=comb.at[blocks + frm], send_sem=cast_s.at[k], recv_sem=cast_r.at[frm],
            device_id={"group": frm}, device_id_type=MESH).wait_recv()
        return 0

    lax.fori_loop(1, groups, cast_wait, 0)
    to_smem.wait()
    keeps = [keep, pltpu.make_async_copy(comb, pool.at[pl.ds(0, held)], near.at[6])]
    keeps[1].start()
    twins = [pltpu.make_async_remote_copy(
        src_ref=comb, dst_ref=pool.at[pl.ds(twin_at, held)], send_sem=twin_s.at[0], recv_sem=twin_r.at[0],
        device_id={"member": twin}, device_id_type=MESH)]

    def ring(way, step):
        at = offset(way, step)
        to = (m + 2) % members if way == 0 else (m + members - 2) % members
        return pltpu.make_async_remote_copy(
            src_ref=sent[way * depth + step], dst_ref=got[way * depth + step],
            send_sem=ring_s.at[way * depth + step], recv_sem=ring_r.at[way * depth + step],
            device_id={"member": to}, device_id_type=MESH)

    def pack(way, step):
        i = way * depth + step
        source, target = (comb if step == 0 else got[i - 1]), sent[i]

        def one(j, _):
            target[j] = source[jnp.clip(route_s[j, i], 0, source.shape[0] - 1)]
            return 0

        lax.fori_loop(0, caps[step], one, 0)
        ring(way, step).start()

    later = [(depth,), (2, chips - 2), (1, chips - 1), ()]

    def over_copy(k):
        to = (g + k) % groups
        return pltpu.make_async_remote_copy(
            src_ref=over, dst_ref=overs.at[g], send_sem=over_s.at[k], recv_sem=over_r.at[g],
            device_id={"group": to}, device_id_type=MESH)

    for step in range(depth):
        for way in range(2):
            i = way * depth + step
            if step > 0:
                ring(way, step - 1).wait_recv()
            pack(way, step)
            if step > 0:
                at, size = offset(way, step - 1), caps[step - 1]
                twins.append(pltpu.make_async_remote_copy(
                    src_ref=got[i - 1], dst_ref=pool.at[pl.ds(ring_twin_at + at, size)],
                    send_sem=twin_s.at[2 + i - 1], recv_sem=twin_r.at[2 + i - 1], device_id={"member": twin}, device_id_type=MESH))
                twins[-1].start()
                keeps.append(pltpu.make_async_copy(got[i - 1], pool.at[pl.ds(ring_at + at, size)], near.at[8 + i - 1]))
                keeps[-1].start()
        own_start(*later[step])
        if step == 0:
            twins[0].start()

            def over_start(k, _):
                over_copy(k).start()
                return 0

            lax.fori_loop(1, groups, over_start, 0)
            alone = pltpu.make_async_copy(over, overs.at[g], near.at[7])
            alone.start()
            own_copy(twin).start()

    def own_wait(k, _):
        frm = (m + k) % members
        pltpu.make_async_remote_copy(
            src_ref=kv_hbm.at[pl.ds(0, own_blocks)], dst_ref=pool.at[pl.ds(own_at + frm * own_blocks, own_blocks)],
            send_sem=own_s.at[frm], recv_sem=own_r.at[frm], device_id={"member": frm}, device_id_type=MESH).wait_recv()
        return 0

    lax.fori_loop(1, members, own_wait, 0)
    keep.wait()
    twins.append(pltpu.make_async_remote_copy(
        src_ref=pool.at[pl.ds(own_at, blocks)], dst_ref=pool.at[pl.ds(own_twin_at, blocks)],
        send_sem=twin_s.at[1], recv_sem=twin_r.at[1], device_id={"member": twin}, device_id_type=MESH))
    twins[-1].start()

    def over_wait(k, _):
        frm = (g + k) % groups
        pltpu.make_async_remote_copy(
            src_ref=over, dst_ref=overs.at[frm], send_sem=over_s.at[k], recv_sem=over_r.at[frm],
            device_id={"group": frm}, device_id_type=MESH).wait_recv()
        return 0

    lax.fori_loop(1, groups, over_wait, 0)
    alone.wait()
    full_flag[0, 0] = jnp.max(overs[...].astype(jnp.float32)).astype(jnp.int32)

    for way in range(2):
        i = way * depth + depth - 1
        at, size = offset(way, depth - 1), caps[depth - 1]
        ring(way, depth - 1).wait_recv()
        twins.append(pltpu.make_async_remote_copy(
            src_ref=got[i], dst_ref=pool.at[pl.ds(ring_twin_at + at, size)],
            send_sem=twin_s.at[2 + i], recv_sem=twin_r.at[2 + i], device_id={"member": twin}, device_id_type=MESH))
        twins[-1].start()
        keeps.append(pltpu.make_async_copy(got[i], pool.at[pl.ds(ring_at + at, size)], near.at[8 + i]))
        keeps[-1].start()

    def drain(k, _):
        list_copy(k).wait_send()
        own_copy((m + k) % members).wait_send()
        return 0

    def drain_group(k, _):
        cast_copy(k).wait_send()
        over_copy(k).wait_send()
        return 0

    lax.fori_loop(1, members, drain, 0)
    lax.fori_loop(1, groups, drain_group, 0)
    for way in range(2):
        for step in range(depth):
            ring(way, step).wait_send()
    for copy in twins:
        copy.wait()
    for copy in keeps[1:]:
        copy.wait()


def spread(caps, collective_id, keys_values, local_lists, remote_lists, targets):
    blocks, share, width = keys_values.shape
    groups, members = targets.shape[1], 16
    chips, depth = members // 2, len(caps)
    held, total = blocks + groups, sum(caps)
    units = 2 * held + 2 * blocks + 4 * total
    unit = (share, width)
    dma = pltpu.SemaphoreType.DMA
    rings = [pltpu.VMEM((cap,) + unit, jnp.bfloat16) for _ in range(2) for cap in caps]
    depth_pad = -(-max(caps) // 8) * 8

    def kernel(*refs):
        lead, rings_at = 17, 17 + 2 * depth
        spread_kernel(caps, *refs[:lead], refs[lead:rings_at], refs[rings_at:rings_at + 2 * depth], *refs[rings_at + 2 * depth:])

    return pl.pallas_call(
        kernel,
        out_shape=(jax.ShapeDtypeStruct((units,) + unit, jnp.bfloat16),
                   jax.ShapeDtypeStruct((members, 128), jnp.int32),
                   jax.ShapeDtypeStruct((1, 1), jnp.int32)),
        in_specs=[pl.BlockSpec(memory_space=pl.ANY)] + [pl.BlockSpec(memory_space=pltpu.SMEM)] * 3,
        out_specs=(pl.BlockSpec(memory_space=pl.ANY), pl.BlockSpec(memory_space=pltpu.VMEM),
                   pl.BlockSpec(memory_space=pltpu.SMEM)),
        scratch_shapes=[
            pltpu.VMEM((16, 128), jnp.int32),
            pltpu.VMEM((blocks,) + unit, jnp.bfloat16),
            pltpu.VMEM((held,) + unit, jnp.bfloat16),
            pltpu.VMEM((groups,) + unit, jnp.bfloat16),
            pltpu.VMEM((chips, 2, 16, 128), jnp.int32),
            pltpu.VMEM((chips, 128), jnp.float32),
            pltpu.VMEM((depth_pad, 128), jnp.int32),
            pltpu.SMEM((depth_pad, 128), jnp.int32),
            pltpu.VMEM((8, 128), jnp.int32),
            pltpu.VMEM((groups, 8, 128), jnp.int32),
        ] + rings + rings + [
            dma((members,)), dma((members,)), dma((groups,)), dma((groups,)), dma((members,)), dma((members,)),
            dma((groups,)), dma((groups,)), dma((2 * depth,)), dma((2 * depth,)), dma((2 + 2 * depth,)), dma((2 + 2 * depth,)),
            dma((8 + 2 * depth,)),
        ],
        compiler_params=pltpu.CompilerParams(
            collective_id=collective_id, has_side_effects=True, vmem_limit_bytes=60 << 20),
        name="spread",
    )(keys_values, local_lists, remote_lists, targets)


FEW = (30, 26, 20, 11)


def shards(queries, keys_values, local_lists, remote_lists, send_blocks):
    blocks, groups = keys_values.shape[0], send_blocks.shape[1]
    pool, table, over = spread(FEW, 0, keys_values, local_lists, remote_lists, send_blocks)

    def enough():
        return attend(local_lists, remote_lists, table, queries, pool)

    def whole():
        held = blocks + groups
        pool, table, _ = spread((held, held, held, held // 2), 1, keys_values, local_lists, remote_lists, send_blocks)
        return attend(local_lists, remote_lists, table, queries, pool)

    return lax.cond(over[0, 0] > 0, whole, enough)


def solution(mesh):
    placed = (
        P(("group", "member"), None),
        P("group", "member", None),
        P(("group", "member"), None),
        P(("group", "member"), None),
        P("group", None),
    )
    return jax.shard_map(
        shards, mesh=mesh, in_specs=placed, out_specs=P(("group", "member"), None), check_vma=False
    )
```

```python
import functools

import jax
import jax.numpy as jnp
from jax import lax
from jax.experimental import pallas as pl
from jax.experimental.pallas import tpu as pltpu
from jax.sharding import PartitionSpec as P

MESH = pl.DeviceIdType.MESH
DIRECT = (1, 3)
HEADS, KV_HEADS, HEAD_DIM = 48, 8, 128
CH = 6
REPEAT = HEADS // KV_HEADS
SCALE = HEAD_DIM ** -0.5 * 1.4426950408889634


def attend_kernel(local_ref, remote_ref, table_ref, q_ref, pool, out_ref, kv, scores_a, scores_b, weights_a, weights_b, sems):
    scores, weights = (scores_a, scores_b), (weights_a, weights_b)
    block = pl.program_id(0)
    n_local, n_remote = local_ref.shape[1], remote_ref.shape[1]
    rows = q_ref.shape[0]
    keys = kv.shape[1] // (n_local + n_remote)
    members = keys // 8

    def counts(b):
        near = sum((local_ref[b, i] >= 0).astype(jnp.int32) for i in range(n_local))
        far = sum((remote_ref[b, i] >= 0).astype(jnp.int32) for i in range(n_remote))
        return near, far

    near, far = counts(block)
    total = near + far
    pairs = lax.div(total + 1, 2)

    def fetch(b):
        near, far = counts(b)
        total = near + far
        last = total + lax.rem(total, 2)

        def slot_copies(s, _):
            part = jnp.where(s < near, local_ref[b, jnp.minimum(s, n_local - 1)],
                             remote_ref[b, jnp.clip(s - near, 0, n_remote - 1)] + 32)
            which = jnp.where(s < total, part, local_ref[b, 0])
            for m in range(members):
                pltpu.make_async_copy(
                    pool.at[table_ref[m, which]],
                    kv.at[b, pl.ds(pl.multiple_of(s * keys + m * 8, 8), 8), :], sems.at[b]).start()
            return 0

        lax.fori_loop(0, last, slot_copies, 0)

    @pl.when(block == 0)
    def _():
        for b in range(kv.shape[0]):
            fetch(b)

    def drain(s, _):
        pltpu.make_async_copy(
            kv.at[block, pl.ds(0, 2 * keys), :], kv.at[block, pl.ds(0, 2 * keys), :], sems.at[block]).wait()
        return 0

    lax.fori_loop(0, pairs, drain, 0)

    share = REPEAT // 2

    def work(pairs):
        bias = jnp.where(2 * pairs == total, 0.0, -jnp.inf)

        def column(head, part, r):
            return pl.ds(pl.multiple_of((head * REPEAT + part * share + r) * HEAD_DIM, HEAD_DIM), HEAD_DIM)

        def score(head, part):
            q = jnp.concatenate([q_ref[:, column(head, part, r)] for r in range(share)], axis=0)
            for j in range(pairs):
                k = kv[block, j * 2 * keys:(j + 1) * 2 * keys, pl.ds(pl.multiple_of(head * HEAD_DIM, HEAD_DIM), HEAD_DIM)]
                scores[part][j] = lax.dot_general(q, k, (((1,), (1,)), ((), ())), preferred_element_type=jnp.float32)

        def weigh(part):
            for r in range(share):
                span = slice(r * rows, (r + 1) * rows)
                parts = []
                for j in range(pairs):
                    parts.append(scores[part][j, span, :keys])
                    last = scores[part][j, span, keys:]
                    parts.append(last + bias if j == pairs - 1 else last)
                top = functools.reduce(jnp.maximum, parts)
                top = jnp.max(top, axis=1, keepdims=True) * SCALE
                for i, piece in enumerate(parts):
                    weights[part][span, i * keys:(i + 1) * keys] = jnp.exp2(piece * SCALE - top).astype(jnp.bfloat16)

        def mix(head, part):
            at = pl.multiple_of((KV_HEADS + head) * HEAD_DIM, HEAD_DIM)
            v = kv[block, :pairs * 2 * keys, pl.ds(at, HEAD_DIM)]
            both = jnp.concatenate([v, jnp.ones((pairs * 2 * keys, HEAD_DIM), jnp.bfloat16)], axis=1)
            acc = jnp.concatenate([
                jnp.dot(weights[part][h:h + share * rows // 2, :pairs * 2 * keys], both, preferred_element_type=jnp.float32)
                for h in range(0, share * rows, share * rows // 2)], axis=0)
            out = (acc[:, :HEAD_DIM] / acc[:, HEAD_DIM:]).astype(jnp.bfloat16)
            for r in range(share):
                out_ref[:, column(head, part, r)] = out[r * rows:(r + 1) * rows]

        def step(head, _):
            score(head, 1)
            weigh(0)
            mix(jnp.maximum(head - 1, 0), 1)
            score(jnp.minimum(head + 1, KV_HEADS - 1), 0)
            weigh(1)
            mix(head, 0)
            return 0

        score(0, 0)
        lax.fori_loop(0, KV_HEADS, step, 0)
        mix(KV_HEADS - 1, 1)

    for count in range(1, kv.shape[1] // (2 * keys) + 1):
        pl.when(pairs == count)(functools.partial(work, count))


def attend(local_lists, remote_lists, table, queries, pool):
    blocks = local_lists.shape[0]
    rows = queries.shape[0] // blocks
    slots = local_lists.shape[1] + remote_lists.shape[1]
    keys = 128
    return pl.pallas_call(
        attend_kernel,
        out_shape=jax.ShapeDtypeStruct(queries.shape, jnp.bfloat16),
        grid_spec=pltpu.PrefetchScalarGridSpec(
            num_scalar_prefetch=3, grid=(blocks,),
            in_specs=[pl.BlockSpec((rows, queries.shape[1]), lambda b, *_: (b, 0)),
                      pl.BlockSpec(memory_space=pl.ANY)],
            out_specs=pl.BlockSpec((rows, queries.shape[1]), lambda b, *_: (b, 0)),
            scratch_shapes=[
                pltpu.VMEM((blocks, slots * keys, 2 * KV_HEADS * HEAD_DIM), jnp.bfloat16),
                pltpu.VMEM((slots // 2, REPEAT // 2 * rows, 2 * keys), jnp.float32),
                pltpu.VMEM((slots // 2, REPEAT // 2 * rows, 2 * keys), jnp.float32),
                pltpu.VMEM((REPEAT // 2 * rows, slots * keys), jnp.bfloat16),
                pltpu.VMEM((REPEAT // 2 * rows, slots * keys), jnp.bfloat16),
                pltpu.SemaphoreType.DMA((blocks,)),
            ]),
        compiler_params=pltpu.CompilerParams(
            vmem_limit_bytes=62 << 20),
        name="attend",
    )(local_lists, remote_lists, table, queries, pool)


def spread_kernel(caps, kv_hbm, local_ref, remote_ref, targets, pool, table, full_flag, entries, kvv, comb, outgoing, lists, need, route, route_s,
                  over, overs, sent, got, own_s, own_r, cast_s, cast_r, list_s, list_r, over_s, over_r, ring_s, ring_r,
                  twin_s, twin_r, near):
    g, m = lax.axis_index("group"), lax.axis_index("member")
    groups, members, depth = comb.shape[0] - kvv.shape[0], lists.shape[0] * 2, len(caps)
    blocks, chips = kvv.shape[0], lists.shape[0]
    held = blocks + groups
    own_blocks = blocks // members
    z, c = m // 2, m % 2
    twin = z * 2 + (1 - c)
    total = sum(caps)
    twin_at, own_at, own_twin_at = held, 2 * held, 2 * held + blocks
    ring_at = 2 * held + 2 * blocks
    ring_twin_at = ring_at + 2 * total

    def offset(way, step):
        return way * total + sum(caps[:step])

    n_local, n_remote = local_ref.shape[1], remote_ref.shape[1]
    for b in range(local_ref.shape[0]):
        for i in range(n_local):
            entries[b * n_local + i:b * n_local + i + 1, :] = jnp.full((1, 128), local_ref[b, i], jnp.int32)
        for i in range(n_remote):
            at = local_ref.shape[0] * n_local + b * n_remote + i
            other = remote_ref[b, i]
            entries[at:at + 1, :] = jnp.full((1, 128), jnp.where(other >= 0, other + blocks, -1), jnp.int32)

    loads = [pltpu.make_async_copy(kv_hbm, kvv, near.at[0]),
             pltpu.make_async_copy(kv_hbm, comb.at[pl.ds(0, blocks)], near.at[1]),
             pltpu.make_async_copy(entries, lists.at[0, c], near.at[2])]
    loads[0].start()
    loads[1].start()

    barrier = pltpu.get_barrier_semaphore()

    def greet(k, _):
        pl.semaphore_signal(barrier, inc=1, device_id={"member": (m + k) % members}, device_id_type=MESH)
        return 0

    def greet_group(k, _):
        pl.semaphore_signal(barrier, inc=1, device_id={"group": (g + k) % groups}, device_id_type=MESH)
        return 0

    lax.fori_loop(1, members, greet, 0)
    lax.fori_loop(1, groups, greet_group, 0)
    pl.semaphore_wait(barrier, members + groups - 2)

    def list_copy(k):
        to = (m + k) % members
        slot = (z - to // 2 + chips) % chips
        return pltpu.make_async_remote_copy(
            src_ref=entries, dst_ref=lists.at[slot, c], send_sem=list_s.at[k], recv_sem=list_r.at[slot * 2 + c],
            device_id={"member": to}, device_id_type=MESH)

    def list_start(k, _):
        list_copy(k).start()
        return 0

    loads[2].start()
    lax.fori_loop(1, members, list_start, 0)

    loads[0].wait()

    def pick(i, _):
        outgoing[i] = kvv[targets[0, i]]
        return 0

    lax.fori_loop(0, groups, pick, 0)

    def cast_copy(k):
        to = (g + k) % groups
        return pltpu.make_async_remote_copy(
            src_ref=outgoing.at[to], dst_ref=comb.at[blocks + g], send_sem=cast_s.at[k], recv_sem=cast_r.at[g],
            device_id={"group": to}, device_id_type=MESH)

    def cast_start(k, _):
        cast_copy(k).start()
        return 0

    lax.fori_loop(1, groups, cast_start, 0)
    loads.append(pltpu.make_async_copy(outgoing.at[g], comb.at[blocks + g], near.at[3]))
    loads[3].start()

    def own_copy(to):
        return pltpu.make_async_remote_copy(
            src_ref=kv_hbm.at[pl.ds(to * own_blocks, own_blocks)],
            dst_ref=pool.at[pl.ds(own_at + m * own_blocks, own_blocks)],
            send_sem=own_s.at[to], recv_sem=own_r.at[m], device_id={"member": to}, device_id_type=MESH)

    def own_start(shifts, cores):
        for shift in shifts:
            for core in cores:
                own_copy((z + shift) % chips * 2 + core).start()

    own_start((3, chips - 3), (0, 1))

    def list_wait(k, _):
        frm = (m + k) % members
        slot = (frm // 2 - z + chips) % chips
        pltpu.make_async_remote_copy(
            src_ref=entries, dst_ref=lists.at[slot, frm % 2], send_sem=list_s.at[k],
            recv_sem=list_r.at[slot * 2 + frm % 2], device_id={"member": frm}, device_id_type=MESH).wait_recv()
        return 0

    loads[2].wait()
    lax.fori_loop(1, members, list_wait, 0)
    lane = lax.broadcasted_iota(jnp.int32, (16, 128), 1)
    for k in range(chips):
        found = jnp.maximum(jnp.where(lists[k, 0] == lane, 1.0, 0.0), jnp.where(lists[k, 1] == lane, 1.0, 0.0))
        need[k:k + 1, :] = jnp.max(found, axis=0, keepdims=True)
    lane = lax.broadcasted_iota(jnp.int32, (chips, 128), 1)
    chip = (lax.broadcasted_iota(jnp.int32, (chips, 128), 0) + z) % chips
    own_width = 2 * own_blocks
    mine = jnp.logical_and(lane >= chip * own_width, lane < chip * own_width + own_width)
    wanted = jnp.where(mine, 0.0, need[...])
    even = jnp.where(lane % 2 == 0, 1.0, 0.0)
    wants = []
    for way in range(2):
        rest = [pltpu.roll(wanted, (chips - d if way == 0 else d) % chips, 0) for d in range(depth + 1)]
        full = [pltpu.roll(need[...], (chips - d if way == 0 else d) % chips, 0) for d in range(depth + 1)]
        half = even if way == 0 else 1.0 - even
        for step in range(depth):
            far = depth - step
            ahead = [(rest if k + step in DIRECT else full)[k] for k in range(far + 1)]
            flags = ahead[far] * half
            for k in range(1, far):
                flags = jnp.maximum(flags, ahead[k])
            wants.append(flags)
    lower = jnp.where(lax.broadcasted_iota(jnp.int32, (128, 128), 0) < lax.broadcasted_iota(jnp.int32, (128, 128), 1), 1.0, 0.0)
    stacked = jnp.concatenate(wants, axis=0)
    places = jnp.dot(stacked.astype(jnp.bfloat16), lower.astype(jnp.bfloat16), preferred_element_type=jnp.float32)
    places = [places[i * chips:(i + 1) * chips] for i in range(2 * depth)]
    lane_row = lax.broadcasted_iota(jnp.int32, (1, 128), 1)
    slot_ids = lax.broadcasted_iota(jnp.int32, route.shape, 0).astype(jnp.float32)
    columns = lax.broadcasted_iota(jnp.int32, route.shape, 1)
    picks = jnp.zeros(route.shape, jnp.float32)
    too_many = jnp.zeros((chips, 1), jnp.float32)
    for way in range(2):
        source = chips - 1 if way == 0 else 1
        for step in range(depth):
            i = way * depth + step
            flags, place = wants[i][0:1], places[i][0:1]
            value = lane_row.astype(jnp.float32) if step == 0 else places[i - 1][source:source + 1]
            hit = jnp.where(place == slot_ids, flags * value, 0.0)
            picks = jnp.where(columns == i, jnp.sum(hit, axis=1, keepdims=True), picks)
            count = jnp.sum(wants[i], axis=1, keepdims=True)
            too_many = jnp.maximum(too_many, jnp.where(count > caps[step], 1.0, 0.0))
    route[...] = picks.astype(jnp.int32)
    to_smem = pltpu.make_async_copy(route, route_s, near.at[5])
    to_smem.start()
    over[...] = jnp.broadcast_to(jnp.max(too_many, axis=0, keepdims=True), over.shape).astype(jnp.int32)

    core_block = lane_row // own_blocks
    for k in range(chips):
        zz = (z + k) % chips
        for t in range(2):
            if k == 0:
                row = lane_row + t * twin_at
            else:
                base = ring_at if t == 0 else ring_twin_at
                plus = places[min(chips - k, depth) - 1][chips - 1:chips].astype(jnp.int32) + base + offset(0, min(chips - k, depth) - 1)
                minus = places[depth + min(k, depth) - 1][1:2].astype(jnp.int32) + base + offset(1, min(k, depth) - 1)
                if k < depth:
                    row = minus
                elif k > depth:
                    row = plus
                else:
                    row = jnp.where(lane_row % 2 == 0, plus, minus)
                member = zz * 2 + (c if t == 0 else 1 - c)
                if min(k, chips - k) in DIRECT:
                    row = jnp.where(core_block == m, own_at + member * own_blocks + lane_row - m * own_blocks, row)
                    row = jnp.where(core_block == twin, own_twin_at + member * own_blocks + lane_row - twin * own_blocks, row)
            table[2 * k + t:2 * k + t + 1, :] = row

    loads[1].wait()
    loads[3].wait()

    def cast_wait(k, _):
        frm = (g + k) % groups
        pltpu.make_async_remote_copy(
            src_ref=outgoing.at[frm], dst_ref=comb.at[blocks + frm], send_sem=cast_s.at[k], recv_sem=cast_r.at[frm],
            device_id={"group": frm}, device_id_type=MESH).wait_recv()
        return 0

    lax.fori_loop(1, groups, cast_wait, 0)
    to_smem.wait()
    keeps = [pltpu.make_async_copy(comb, pool.at[pl.ds(0, held)], near.at[6])]
    keeps[0].start()
    twins = [pltpu.make_async_remote_copy(
        src_ref=comb, dst_ref=pool.at[pl.ds(twin_at, held)], send_sem=twin_s.at[0], recv_sem=twin_r.at[0],
        device_id={"member": twin}, device_id_type=MESH)]

    def ring(way, step):
        at = offset(way, step)
        to = (m + 2) % members if way == 0 else (m + members - 2) % members
        return pltpu.make_async_remote_copy(
            src_ref=sent[way * depth + step], dst_ref=got[way * depth + step],
            send_sem=ring_s.at[way * depth + step], recv_sem=ring_r.at[way * depth + step],
            device_id={"member": to}, device_id_type=MESH)

    def pack(way, step):
        i = way * depth + step
        source, target = (comb if step == 0 else got[i - 1]), sent[i]

        def one(j, _):
            target[j] = source[jnp.clip(route_s[j, i], 0, source.shape[0] - 1)]
            return 0

        lax.fori_loop(0, caps[step], one, 0)
        ring(way, step).start()

    later = [(0,), (1,)] + [()] * (depth - 2)

    def over_copy(k):
        to = (g + k) % groups
        return pltpu.make_async_remote_copy(
            src_ref=over, dst_ref=overs.at[g], send_sem=over_s.at[k], recv_sem=over_r.at[g],
            device_id={"group": to}, device_id_type=MESH)

    for step in range(depth):
        for way in range(2):
            i = way * depth + step
            if step > 0:
                ring(way, step - 1).wait_recv()
            pack(way, step)
            if step > 0:
                at, size = offset(way, step - 1), caps[step - 1]
                twins.append(pltpu.make_async_remote_copy(
                    src_ref=got[i - 1], dst_ref=pool.at[pl.ds(ring_twin_at + at, size)],
                    send_sem=twin_s.at[2 + i - 1], recv_sem=twin_r.at[2 + i - 1], device_id={"member": twin}, device_id_type=MESH))
                twins[-1].start()
                keeps.append(pltpu.make_async_copy(got[i - 1], pool.at[pl.ds(ring_at + at, size)], near.at[8 + i - 1]))
                keeps[-1].start()
        own_start((1, chips - 1), later[step])
        if step == 0:
            twins[0].start()

            def over_start(k, _):
                over_copy(k).start()
                return 0

            lax.fori_loop(1, groups, over_start, 0)
            alone = pltpu.make_async_copy(over, overs.at[g], near.at[7])
            alone.start()

    for i, shift in enumerate((3, chips - 3, 1, chips - 1)):
        chip_from = (z + shift) % chips
        for core in range(2):
            frm = chip_from * 2 + core
            pltpu.make_async_remote_copy(
                src_ref=kv_hbm.at[pl.ds(0, own_blocks)], dst_ref=pool.at[pl.ds(own_at + frm * own_blocks, own_blocks)],
                send_sem=own_s.at[frm], recv_sem=own_r.at[frm], device_id={"member": frm}, device_id_type=MESH).wait_recv()
        twins.append(pltpu.make_async_remote_copy(
            src_ref=pool.at[pl.ds(own_at + chip_from * 2 * own_blocks, 2 * own_blocks)],
            dst_ref=pool.at[pl.ds(own_twin_at + chip_from * 2 * own_blocks, 2 * own_blocks)],
            send_sem=twin_s.at[2 + 2 * depth + i], recv_sem=twin_r.at[2 + 2 * depth + i],
            device_id={"member": twin}, device_id_type=MESH))
        twins[-1].start()

    def over_wait(k, _):
        frm = (g + k) % groups
        pltpu.make_async_remote_copy(
            src_ref=over, dst_ref=overs.at[frm], send_sem=over_s.at[k], recv_sem=over_r.at[frm],
            device_id={"group": frm}, device_id_type=MESH).wait_recv()
        return 0

    lax.fori_loop(1, groups, over_wait, 0)
    alone.wait()
    full_flag[0, 0] = jnp.max(overs[...].astype(jnp.float32)).astype(jnp.int32)

    for way in range(2):
        i = way * depth + depth - 1
        at, size = offset(way, depth - 1), caps[depth - 1]
        ring(way, depth - 1).wait_recv()
        twins.append(pltpu.make_async_remote_copy(
            src_ref=got[i], dst_ref=pool.at[pl.ds(ring_twin_at + at, size)],
            send_sem=twin_s.at[2 + i], recv_sem=twin_r.at[2 + i], device_id={"member": twin}, device_id_type=MESH))
        twins[-1].start()
        keeps.append(pltpu.make_async_copy(got[i], pool.at[pl.ds(ring_at + at, size)], near.at[8 + i]))
        keeps[-1].start()

    def drain(k, _):
        list_copy(k).wait_send()
        return 0

    def drain_group(k, _):
        cast_copy(k).wait_send()
        over_copy(k).wait_send()
        return 0

    lax.fori_loop(1, members, drain, 0)
    lax.fori_loop(1, groups, drain_group, 0)
    for shift in (3, chips - 3, 1, chips - 1):
        for core in range(2):
            own_copy((z + shift) % chips * 2 + core).wait_send()
    for way in range(2):
        for step in range(depth):
            ring(way, step).wait_send()
    for copy in twins:
        copy.wait()
    for copy in keeps:
        copy.wait()


def spread(caps, collective_id, keys_values, local_lists, remote_lists, targets):
    blocks, share, width = keys_values.shape
    groups, members = targets.shape[1], 16
    chips, depth = members // 2, len(caps)
    held, total = blocks + groups, sum(caps)
    units = 2 * held + 2 * blocks + 4 * total
    unit = (share, width)
    dma = pltpu.SemaphoreType.DMA
    rings = [pltpu.VMEM((cap,) + unit, jnp.bfloat16) for _ in range(2) for cap in caps]
    depth_pad = -(-max(caps) // 8) * 8

    def kernel(*refs):
        lead, rings_at = 17, 17 + 2 * depth
        spread_kernel(caps, *refs[:lead], refs[lead:rings_at], refs[rings_at:rings_at + 2 * depth], *refs[rings_at + 2 * depth:])

    return pl.pallas_call(
        kernel,
        out_shape=(jax.ShapeDtypeStruct((units,) + unit, jnp.bfloat16),
                   jax.ShapeDtypeStruct((members, 128), jnp.int32),
                   jax.ShapeDtypeStruct((1, 1), jnp.int32)),
        in_specs=[pl.BlockSpec(memory_space=pl.ANY)] + [pl.BlockSpec(memory_space=pltpu.SMEM)] * 3,
        out_specs=(pl.BlockSpec(memory_space=pl.ANY), pl.BlockSpec(memory_space=pltpu.VMEM),
                   pl.BlockSpec(memory_space=pltpu.SMEM)),
        scratch_shapes=[
            pltpu.VMEM((16, 128), jnp.int32),
            pltpu.VMEM((blocks,) + unit, jnp.bfloat16),
            pltpu.VMEM((held,) + unit, jnp.bfloat16),
            pltpu.VMEM((groups,) + unit, jnp.bfloat16),
            pltpu.VMEM((chips, 2, 16, 128), jnp.int32),
            pltpu.VMEM((chips, 128), jnp.float32),
            pltpu.VMEM((depth_pad, 128), jnp.int32),
            pltpu.SMEM((depth_pad, 128), jnp.int32),
            pltpu.VMEM((8, 128), jnp.int32),
            pltpu.VMEM((groups, 8, 128), jnp.int32),
        ] + rings + rings + [
            dma((members,)), dma((members,)), dma((groups,)), dma((groups,)), dma((members,)), dma((members,)),
            dma((groups,)), dma((groups,)), dma((2 * depth,)), dma((2 * depth,)), dma((6 + 2 * depth,)), dma((6 + 2 * depth,)),
            dma((8 + 2 * depth,)),
        ],
        compiler_params=pltpu.CompilerParams(
            collective_id=collective_id, has_side_effects=True, vmem_limit_bytes=60 << 20),
        name="spread",
    )(keys_values, local_lists, remote_lists, targets)


FEW = (33, 31, 22, 13)


def shards(queries, keys_values, local_lists, remote_lists, send_blocks):
    blocks, groups = keys_values.shape[0], send_blocks.shape[1]
    pool, table, over = spread(FEW, 0, keys_values, local_lists, remote_lists, send_blocks)

    def enough():
        return attend(local_lists, remote_lists, table, queries, pool)

    def whole():
        held = blocks + groups
        pool, table, _ = spread((held, held, held, held // 2), 1, keys_values, local_lists, remote_lists, send_blocks)
        return attend(local_lists, remote_lists, table, queries, pool)

    return lax.cond(over[0, 0] > 0, whole, enough)


def solution(mesh):
    placed = (
        P(("group", "member"), None),
        P("group", "member", None),
        P(("group", "member"), None),
        P(("group", "member"), None),
        P("group", None),
    )
    return jax.shard_map(
        shards, mesh=mesh, in_specs=placed, out_specs=P(("group", "member"), None), check_vma=False
    )
```
